32 devices in a mesh: groups: 2 (over x), expert: 16 (over z, y, core).
Axes of the slice: x: 2, y: 2, z: 4, core: 2. Of those that a mesh axis runs over, the one named last changes fastest.
Arguments:
- hidden_in: bfloat16 [256, 4096], P(('groups', 'expert')), parts along dimension 0, may hold values from -6 to 6
- queries: bfloat16 [256, 4096], P(('groups', 'expert')), parts along dimension 0, may hold values from -8 to 8
- decode_key_value: bfloat16 [256, 2, 256], P(('groups', 'expert')), parts along dimension 0, may hold values from -6 to 6
- local_kv: bfloat16 [1024, 2, 16, 256], P(('groups', 'expert')), parts along dimension 0, may hold values from -8 to 8
- page_table: int32 [256, 16], P(('groups', 'expert')), parts along dimension 0, may hold values from 0 to 31
- seq_blocks: int32 [256], P(('groups', 'expert')), parts along dimension 0, may hold values from 1 to 16
- prompt_kv: bfloat16 [32, 16, 2, 16, 256], P(('groups', 'expert')), parts along dimension 0, may hold values from -8 to 8
- prompt_owner: int32 [32], P('groups'), parts along dimension 0, may hold values from 0 to 15, as said below
- prompt_pages: int32 [32], P('groups'), parts along dimension 0, may hold values from 1 to 16
- norm_gain: float32 [4096], replicated, may hold values from 0.5 to 1.5
- router: bfloat16 [4096, 8], replicated, may hold values from -0.09375 to 0.09375
- w_gate: bfloat16 [16, 4096, 384], P('expert'), may hold values from -0.09375 to 0.09375
- w_up: bfloat16 [16, 4096, 384], P('expert'), may hold values from -0.09375 to 0.09375
- w_down: bfloat16 [16, 384, 4096], P('expert'), may hold values from -0.21875 to 0.21875
- route_ids: int32 [256, 8], P(('groups', 'expert')), parts along dimension 0, may hold values from 0 to 7, as said below
Outputs:
- layer_out: bfloat16 [256, 4096], P(('groups', 'expert')), parts along dimension 0
The draws below stay inside these ranges and needn't reach their ends.
There are 2 independent parts, one for each index of `groups`. The reference program is written for one: setup_inputs(seed, part) draws one part's arguments, and reference() takes and returns one part's arrays. A program takes and returns all parts, laid end to end along the dimension named above; an argument that names none is the same for every part. Nothing has to cross between parts.
Inputs may be any that keep to these rules, and one draw needn't show every extreme that they name: `prompt_owner`: each device is named by at most 2 prompts, and by exactly 2 for some of the devices. `route_ids`: each row names 8 different experts; among the rows of one device no expert is named more than 8 times, a bound that some block reaches. `page_table`: indices among the pages of the sequence's own device.
All inputs are finite; a program needn't handle non-finite values.
Results may differ from the reference program's by a relative error of at most 0.0056.
Values may be sent and summed in bfloat16 or wider, within the bound.
No kernel may reach another device: no remote copies, remote signals or barrier semaphores. Data moves between devices by JAX's collectives and lax.ppermute only.
A program may use at most 128 MiB of HBM per device.

```python
import math
import jax
import jax.numpy as jnp
from jax import lax

D = 4096
QUERY_HEADS = 32
KEY_VALUE_HEADS = 2
HEAD_SIZE = 128
PAGE_TOKENS = 16
FW = 768
TOPK = 8
SEQ_DEV = 8
LOCAL_PAGES = 32
MAXB = 16
MAXP = 2
EXPERTS = 8
DECODE_SEQUENCES = 128
PROMPTS = 16
PROMPT_PAGES = 16
CAP = 8
N_EXPERT = 16


def draw_prompt_owner(key, part):
    owner_key, shuffle_key = jax.random.split(jax.random.fold_in(key, 11))
    owners = jax.random.permutation(owner_key, N_EXPERT)
    quarter = N_EXPERT // 4
    listed = jnp.concatenate([owners[:quarter], owners[:quarter], owners[quarter:3 * quarter]])
    shuffle = jax.random.permutation(shuffle_key, N_EXPERT)
    return listed[shuffle].astype(jnp.int32)


def draw_route_ids(key, part):
    device_keys = jax.random.split(jax.random.fold_in(key, 13), N_EXPERT)
    orders = jax.vmap(lambda single: jax.random.permutation(single, EXPERTS))(device_keys)
    window = max(TOPK, (SEQ_DEV * TOPK + CAP - 1) // CAP)
    columns = jnp.arange(SEQ_DEV * TOPK, dtype=jnp.int32) % window
    picked = jnp.take(orders, columns, axis=1)
    return picked.reshape(N_EXPERT * SEQ_DEV, TOPK).astype(jnp.int32)


def common_direction(key):
    random_signs = jax.random.randint(jax.random.fold_in(key, 101), (KEY_VALUE_HEADS * HEAD_SIZE,), 0, 2)
    return (2 * random_signs - 1).astype(jnp.float32)


def starting_noise(key, shape):
    return jnp.clip(jax.random.normal(key, shape, jnp.float32), -6.0, 6.0)


def cache_block(key, salt, leading_share):
    noise_random_key, flag_random_key, strength_random_key, value_random_key = jax.random.split(jax.random.fold_in(key, salt), 4)
    random_noise = starting_noise(noise_random_key, leading_share + (PAGE_TOKENS, KEY_VALUE_HEADS, HEAD_SIZE))
    sign_flags = jax.random.randint(flag_random_key, leading_share + (PAGE_TOKENS, KEY_VALUE_HEADS, 1), 0, 8) == 0
    blend_strength = jax.random.uniform(strength_random_key, leading_share + (PAGE_TOKENS, KEY_VALUE_HEADS, 1), jnp.float32, 5.0, 7.5)
    unit_direction = common_direction(key).reshape(KEY_VALUE_HEADS, HEAD_SIZE)
    cached_keys = jnp.where(sign_flags, 0.3 * random_noise + blend_strength * unit_direction, random_noise)
    cached_keys = jnp.clip(cached_keys, -8.0, 8.0).reshape(leading_share + (PAGE_TOKENS, KEY_VALUE_HEADS * HEAD_SIZE))
    cached_values = starting_noise(value_random_key, leading_share + (PAGE_TOKENS, KEY_VALUE_HEADS * HEAD_SIZE))
    return jnp.stack([cached_keys, cached_values], len(leading_share))


def draw_queries(key, part):
    noise_random_key, flag_random_key, strength_random_key = jax.random.split(jax.random.fold_in(key, 5), 3)
    random_noise = starting_noise(noise_random_key, (DECODE_SEQUENCES, KEY_VALUE_HEADS, QUERY_HEADS // KEY_VALUE_HEADS, HEAD_SIZE))
    sign_flags = jax.random.randint(flag_random_key, (DECODE_SEQUENCES, 1, 1, 1), 0, 4) == 0
    blend_strength = jax.random.uniform(strength_random_key, (DECODE_SEQUENCES, 1, 1, 1), jnp.float32, 2.0, 7.5)
    unit_direction = common_direction(key).reshape(1, KEY_VALUE_HEADS, 1, HEAD_SIZE)
    rows = jnp.where(sign_flags, 0.3 * random_noise + blend_strength * unit_direction, random_noise)
    return jnp.clip(rows, -8.0, 8.0).reshape(DECODE_SEQUENCES, QUERY_HEADS * HEAD_SIZE).astype(jnp.bfloat16)


def draw_local_kv(key, part):
    return cache_block(key, 7, (N_EXPERT * LOCAL_PAGES,)).astype(jnp.bfloat16)


def draw_prompt_kv(key, part):
    return cache_block(key, 8, (PROMPT_PAGES, PROMPTS)).astype(jnp.bfloat16)


def with_ends(drawn, key, smallest, high):
    place = [jax.random.randint(jax.random.fold_in(key, axis), (), 0, length) for axis, length in enumerate(drawn.shape)]
    widest = drawn.shape.index(max(drawn.shape))
    neighbour = place[:widest] + [(place[widest] + 1) % drawn.shape[widest]] + place[widest + 1:]
    return drawn.at[tuple(place)].set(smallest).at[tuple(neighbour)].set(high)


def shard_levels(rng, shape, cuts, least, high):
    gain, own = 1.0, jax.random.fold_in(rng, 6)
    for axis_at, parts in cuts:
        draws = jnp.exp(jax.random.uniform(jax.random.fold_in(own, axis_at), (parts,), jnp.float32, least / len(cuts), high / len(cuts)))
        gain = gain * jnp.repeat(draws, shape[axis_at] // parts).reshape([-1 if axis == axis_at else 1 for axis in range(len(shape))])
    return gain


def bell_draw(stream_key, extent, width, most, cuts=(), kind=jnp.bfloat16):
    values = jax.random.normal(stream_key, extent, jnp.float32) * width
    if len(cuts) > 0:
        values = shard_levels(stream_key, extent, cuts, -0.22, 0.18) * values
    return jnp.clip(values, min=-most, max=most).astype(kind)


def setup_inputs(seed: int = 0, part: int = 0) -> dict:
    splits = jax.random.split(jax.random.key(seed), 16)
    own_keys = jax.random.split(jax.random.fold_in(splits[15], part), 16)
    return {
        "hidden_in": bell_draw(own_keys[0], (DECODE_SEQUENCES, D), 1.0, 6.0, ((0, 16),)),
        "queries": draw_queries(jax.random.fold_in(jax.random.fold_in(splits[15], part), 71), part),
        "decode_key_value": bell_draw(own_keys[2], (DECODE_SEQUENCES, 2, KEY_VALUE_HEADS * HEAD_SIZE), 1.0, 6.0, ((0, 16),)),
        "local_kv": draw_local_kv(jax.random.fold_in(jax.random.fold_in(splits[15], part), 71), part),
        "page_table": with_ends(jax.random.randint(own_keys[4], (DECODE_SEQUENCES, MAXB), 0, LOCAL_PAGES), jax.random.fold_in(own_keys[4], 1), 0, LOCAL_PAGES - 1).astype(jnp.int32),
        "seq_blocks": with_ends(jax.random.randint(own_keys[5], (DECODE_SEQUENCES,), 1, MAXB + 1), jax.random.fold_in(own_keys[5], 1), 1, MAXB).astype(jnp.int32),
        "prompt_kv": draw_prompt_kv(jax.random.fold_in(jax.random.fold_in(splits[15], part), 71), part),
        "prompt_owner": draw_prompt_owner(jax.random.fold_in(jax.random.fold_in(splits[15], part), 71), part),
        "prompt_pages": with_ends(jax.random.randint(own_keys[8], (PROMPTS,), 1, PROMPT_PAGES + 1), jax.random.fold_in(own_keys[8], 1), 1, PROMPT_PAGES).astype(jnp.int32),
        "norm_gain": jnp.clip(1.0 + 0.1 * jax.random.normal(splits[9], (D,), jnp.float32), 0.5, 1.5),
        "router": bell_draw(splits[10], (D, EXPERTS), D ** -0.5, 0.09375),
        "w_gate": bell_draw(splits[11], (2 * EXPERTS, D, FW // 2), D ** -0.5, 0.09375, ((0, 16),)),
        "w_up": bell_draw(splits[12], (2 * EXPERTS, D, FW // 2), D ** -0.5, 0.09375, ((0, 16),)),
        "w_down": bell_draw(splits[13], (2 * EXPERTS, FW // 2, D), FW ** -0.5, 0.21875, ((0, 16),)),
        "route_ids": draw_route_ids(jax.random.fold_in(jax.random.fold_in(splits[15], part), 71), part),
    }


norm_eps = 1e-06
masked_score = -1e+30

def attend(rows_of_queries, rows_of_keys, rows_of_values, allowed, token_own_key, token_own_value):
    decode_tokens = rows_of_queries.shape[0]
    heads_of_queries = rows_of_queries.astype(jnp.float32).reshape(decode_tokens, KEY_VALUE_HEADS, QUERY_HEADS // KEY_VALUE_HEADS, HEAD_SIZE)
    heads_of_keys = rows_of_keys.astype(jnp.float32).reshape(decode_tokens, -1, KEY_VALUE_HEADS, HEAD_SIZE)
    heads_of_values = rows_of_values.astype(jnp.float32).reshape(decode_tokens, -1, KEY_VALUE_HEADS, HEAD_SIZE)
    scale_for_scores = 1.0 / math.sqrt(HEAD_SIZE)
    allowed_mask = allowed[:, None, None, :]
    scores = jnp.einsum('tkgd,tlkd->tkgl', heads_of_queries, heads_of_keys) * scale_for_scores
    scores = jnp.where(allowed_mask, scores, masked_score)
    token_own_score = jnp.einsum('xejp,xep->xej', heads_of_queries, token_own_key.astype(jnp.float32).reshape(decode_tokens, KEY_VALUE_HEADS, HEAD_SIZE)) * scale_for_scores
    peak = jnp.maximum(lax.optimization_barrier(jnp.max(scores, -1)), token_own_score)
    weights = jnp.where(allowed_mask, jnp.exp(scores - peak[..., None]), 0.0)
    own_weight = jnp.exp(token_own_score - peak)
    denominator = lax.optimization_barrier(jnp.sum(weights, -1)) + own_weight
    probs = lax.optimization_barrier((weights / denominator[..., None]).astype(jnp.bfloat16)).astype(jnp.float32)
    token_own_probability = lax.optimization_barrier((own_weight / denominator).astype(jnp.bfloat16)).astype(jnp.float32)
    blended_noise = jnp.einsum('tkgl,tlkd->tkgd', probs, heads_of_values)
    blended_noise = blended_noise + token_own_probability[..., None] * token_own_value.astype(jnp.float32).reshape(decode_tokens, KEY_VALUE_HEADS, 1, HEAD_SIZE)
    return blended_noise.reshape(decode_tokens, QUERY_HEADS * HEAD_SIZE).astype(jnp.bfloat16)

def reference(hidden_in, queries, decode_key_value, local_kv, page_table, seq_blocks, prompt_kv, prompt_owner, prompt_pages, norm_gain, router, w_gate, w_up, w_down, route_ids):
    devices = N_EXPERT
    experts = devices // 2
    key_value_width = KEY_VALUE_HEADS * HEAD_SIZE
    prompt_count = prompt_owner.shape[0]
    prompt_range = jnp.arange(prompt_count, dtype=jnp.int32)
    same_owner = prompt_owner[:, None] == prompt_owner[None, :]
    earlier = prompt_range[None, :] < prompt_range[:, None]
    arrival = lax.optimization_barrier(jnp.sum((same_owner & earlier).astype(jnp.int32), 1))
    matching = (prompt_owner[None, None, :] == jnp.arange(devices, dtype=jnp.int32)[:, None, None]) & (arrival[None, None, :] == jnp.arange(MAXP, dtype=jnp.int32)[None, :, None])
    chosen_prompt = lax.optimization_barrier(jnp.sum(jnp.where(matching, prompt_range[None, None, :], 0), -1)).astype(jnp.int32)
    occupied = jnp.any(matching, -1)

    def owner_attention(inputs):
        owner_index, rows_of_queries, own_kv, pool, table, blocks = inputs
        fetched = pool[table]
        old_keys = fetched[:, :, 0].reshape(SEQ_DEV, MAXB * PAGE_TOKENS, key_value_width)
        old_values = fetched[:, :, 1].reshape(SEQ_DEV, MAXB * PAGE_TOKENS, key_value_width)
        old_allowed = (jnp.arange(MAXB * PAGE_TOKENS, dtype=jnp.int32) // PAGE_TOKENS)[None, :] < blocks[:, None]
        old_out = attend(rows_of_queries, old_keys, old_values, old_allowed, own_kv[:, 0], own_kv[:, 1])
        picks = chosen_prompt[owner_index]
        fresh_pages = jnp.take(prompt_kv, picks, axis=1)
        new_keys = jnp.moveaxis(fresh_pages[:, :, 0], 1, 0).reshape(MAXP, PROMPT_PAGES * PAGE_TOKENS, key_value_width)
        new_values = jnp.moveaxis(fresh_pages[:, :, 1], 1, 0).reshape(MAXP, PROMPT_PAGES * PAGE_TOKENS, key_value_width)
        lengths = prompt_pages[picks]
        new_allowed = (jnp.arange(PROMPT_PAGES * PAGE_TOKENS, dtype=jnp.int32) // PAGE_TOKENS)[None, :] < lengths[:, None]
        new_out = attend(rows_of_queries[:MAXP], new_keys, new_values, new_allowed, own_kv[:MAXP, 0], own_kv[:MAXP, 1])
        new_count = jnp.sum(occupied[owner_index].astype(jnp.int32))
        is_new = jnp.arange(MAXP, dtype=jnp.int32) < new_count
        head_rows = jnp.where(is_new[:, None], new_out, old_out[:MAXP])
        return jnp.concatenate([head_rows, old_out[MAXP:]], 0)
    attention = lax.map(owner_attention, (jnp.arange(devices, dtype=jnp.int32), queries.reshape(devices, SEQ_DEV, QUERY_HEADS * HEAD_SIZE), decode_key_value.reshape(devices, SEQ_DEV, 2, key_value_width), local_kv.reshape(devices, LOCAL_PAGES, 2, PAGE_TOKENS, key_value_width), page_table.reshape(devices, SEQ_DEV, MAXB), seq_blocks.reshape(devices, SEQ_DEV))).reshape(DECODE_SEQUENCES, QUERY_HEADS * HEAD_SIZE)
    residual = (hidden_in.astype(jnp.float32) + attention.astype(jnp.float32)).astype(jnp.bfloat16)
    resid_wide = residual.astype(jnp.float32)
    normed = (resid_wide * lax.rsqrt(lax.optimization_barrier(jnp.mean(resid_wide * resid_wide, -1, keepdims=True)) + norm_eps) * norm_gain).astype(jnp.bfloat16)
    logits = jnp.dot(normed, router, preferred_element_type=jnp.float32)
    selected = jnp.take_along_axis(logits, route_ids, axis=1)
    gate_weights = jax.nn.softmax(selected, -1)
    assigned = SEQ_DEV * TOPK
    expert_ids = route_ids.reshape(devices, assigned)
    chosen = (expert_ids[:, :, None] == jnp.arange(experts, dtype=jnp.int32)[None, None, :]).astype(jnp.int32)
    before = jnp.cumsum(chosen, 1) - chosen
    slot_rank = lax.optimization_barrier(jnp.sum(before * chosen, 2))
    token_index = jnp.arange(devices, dtype=jnp.int32)[:, None] * SEQ_DEV + jnp.arange(assigned, dtype=jnp.int32)[None, :] // TOPK
    gate_flat = gate_weights.reshape(devices, assigned)

    def expert_step(accumulated, expert_index):
        hits = (expert_ids == expert_index)[:, None, :] & (slot_rank[:, None, :] == jnp.arange(CAP, dtype=jnp.int32)[None, :, None])
        present = jnp.any(hits, -1)
        row_token = lax.optimization_barrier(jnp.sum(jnp.where(hits, token_index[:, None, :], 0), -1)).astype(jnp.int32).reshape(-1)
        row_gate = lax.optimization_barrier(jnp.sum(jnp.where(hits, gate_flat[:, None, :], 0.0), -1)).reshape(-1)
        gathered_rows = jnp.where(present.reshape(-1)[:, None], normed[row_token], 0).astype(normed.dtype)
        expert_total = jnp.zeros((devices * CAP, D), jnp.float32)
        for half_index in range(2):
            weight_index = 2 * expert_index + half_index
            gate_proj = jnp.dot(gathered_rows, w_gate[weight_index], preferred_element_type=jnp.float32)
            up_proj = jnp.dot(gathered_rows, w_up[weight_index], preferred_element_type=jnp.float32)
            activated = (jax.nn.silu(gate_proj) * up_proj).astype(jnp.bfloat16)
            expert_total = expert_total + jnp.dot(activated, w_down[weight_index], preferred_element_type=jnp.float32)
        expert_out = lax.optimization_barrier(expert_total.astype(jnp.bfloat16)).astype(jnp.float32)
        accumulated = accumulated.at[row_token].add(expert_out * row_gate[:, None])
        return (accumulated, None)
    accumulated, _ = lax.scan(expert_step, jnp.zeros((DECODE_SEQUENCES, D), jnp.float32), jnp.arange(experts, dtype=jnp.int32))
    return (resid_wide + accumulated).astype(jnp.bfloat16)
```

```python
import math

import jax
import jax.numpy as jnp
from jax import lax
from jax.sharding import PartitionSpec as P

D = 4096
QUERY_HEADS = 32
KEY_VALUE_HEADS = 2
HEAD_SIZE = 128
PAGE_TOKENS = 16
TOPK = 8
MAXB = 16
MAXP = 2


norm_eps = 1e-06
masked_score = -1e30


def partner(x, axis, apart):
    return lax.ppermute(x, axis, [(i, i ^ 1 << apart) for i in range(lax.axis_size(axis))])


def attend(rows_of_queries, rows_of_keys, rows_of_values, allowed, token_own_key, token_own_value):
    decode_tokens = rows_of_queries.shape[0]
    heads_of_queries = rows_of_queries.reshape(
        decode_tokens, KEY_VALUE_HEADS, QUERY_HEADS // KEY_VALUE_HEADS, HEAD_SIZE
    )
    heads_of_keys = rows_of_keys.reshape(decode_tokens, -1, KEY_VALUE_HEADS, HEAD_SIZE)
    heads_of_values = rows_of_values.reshape(decode_tokens, -1, KEY_VALUE_HEADS, HEAD_SIZE)
    scale_for_scores = 1.0 / math.sqrt(HEAD_SIZE)
    allowed_mask = allowed[:, None, None, :]
    scores = (
        jnp.einsum(
            "tkgd,tlkd->tkgl", heads_of_queries, heads_of_keys, preferred_element_type=jnp.float32
        )
        * scale_for_scores
    )
    scores = jnp.where(allowed_mask, scores, masked_score)
    token_own_score = (
        jnp.einsum(
            "xejp,xep->xej",
            heads_of_queries,
            token_own_key.reshape(decode_tokens, KEY_VALUE_HEADS, HEAD_SIZE),
            preferred_element_type=jnp.float32,
        )
        * scale_for_scores
    )
    peak = jnp.maximum(jnp.max(scores, -1), token_own_score)
    weights = jnp.where(allowed_mask, jnp.exp(scores - peak[..., None]), 0.0)
    own_weight = jnp.exp(token_own_score - peak)
    denominator = jnp.sum(weights, -1) + own_weight
    probs = (weights / denominator[..., None]).astype(jnp.bfloat16)
    token_own_probability = (own_weight / denominator).astype(jnp.bfloat16)
    blended_noise = jnp.einsum(
        "tkgl,tlkd->tkgd", probs, heads_of_values, preferred_element_type=jnp.float32
    )
    blended_noise = blended_noise + token_own_probability.astype(jnp.float32)[
        ..., None
    ] * token_own_value.reshape(decode_tokens, KEY_VALUE_HEADS, 1, HEAD_SIZE).astype(jnp.float32)
    return blended_noise.reshape(decode_tokens, QUERY_HEADS * HEAD_SIZE).astype(jnp.bfloat16)


def all_tokens(resid_wide, normed, spread, w_gate, w_up, w_down):
    devices = lax.axis_size("expert")
    seq_dev, experts = spread.shape
    expert = lax.axis_index("expert") // 2
    bits = devices.bit_length() - 1
    coarse = lax.reduce_precision(spread, 8, 7)
    fine = spread - coarse
    pad = -2 * experts % 128
    tail = jnp.pad(jnp.concatenate([coarse, fine], 1), ((0, 0), (0, pad))).astype(jnp.bfloat16)
    rows = jnp.concatenate([normed, tail], 1)
    for bit in reversed(range(bits)):
        rows = jnp.concatenate([rows, partner(rows, "expert", bit)], 0)
    gates = rows[:, D : D + 2 * experts].astype(jnp.float32).reshape(-1, 2, experts)
    own = jnp.arange(experts, dtype=jnp.int32) == expert
    gate = jnp.sum(jnp.where(own, gates, 0.0), (1, 2))
    tokens = rows[:, :D]
    gate_proj = jnp.dot(tokens, w_gate, preferred_element_type=jnp.float32)
    up_proj = jnp.dot(tokens, w_up, preferred_element_type=jnp.float32)
    activated = (jax.nn.silu(gate_proj) * up_proj).astype(jnp.bfloat16)
    mixed = jnp.dot(activated, w_down, preferred_element_type=jnp.float32) * gate[:, None]
    for bit in range(bits):
        half = mixed.shape[0] // 2
        moved = partner(mixed[half:].astype(jnp.bfloat16), "expert", bit)
        mixed = mixed[:half] + moved.astype(jnp.float32)
    return (resid_wide + mixed).astype(jnp.bfloat16)


def local(
    hidden_in,
    queries,
    decode_key_value,
    local_kv,
    page_table,
    seq_blocks,
    prompt_kv,
    prompt_owner,
    prompt_pages,
    norm_gain,
    router,
    w_gate,
    w_up,
    w_down,
    route_ids,
):
    devices = lax.axis_size("expert")
    position = lax.axis_index("expert")
    experts = devices // 2
    seq_dev = hidden_in.shape[0]
    key_value_width = KEY_VALUE_HEADS * HEAD_SIZE
    capacity = min(seq_dev, max(2, 2 * ((3 * seq_dev * TOPK + 2 * devices - 1) // (2 * devices))))
    half_cap = capacity // 2
    even_core = position % 2 == 0
    prompt_count = prompt_owner.shape[0]
    prompt_range = jnp.arange(prompt_count, dtype=jnp.int32)
    same_owner = prompt_owner[:, None] == prompt_owner[None, :]
    earlier = prompt_range[None, :] < prompt_range[:, None]
    arrival = jnp.sum((same_owner & earlier).astype(jnp.int32), 1)
    matching = (
        prompt_owner[None, None, :] == jnp.arange(devices, dtype=jnp.int32)[:, None, None]
    ) & (arrival[None, None, :] == jnp.arange(MAXP, dtype=jnp.int32)[None, :, None])
    chosen_prompt = jnp.sum(jnp.where(matching, prompt_range[None, None, :], 0), -1)
    occupied = jnp.any(matching, -1)
    own_picks = lax.dynamic_index_in_dim(chosen_prompt, position, 0, keepdims=False)
    own_occupied = lax.dynamic_index_in_dim(occupied, position, 0, keepdims=False)
    page_rows = prompt_kv[0]
    outgoing = jnp.take(page_rows, chosen_prompt.T.reshape(-1), axis=0).reshape(
        MAXP, devices, 2, PAGE_TOKENS, key_value_width
    )
    outgoing = jnp.where(occupied.T[:, :, None, None, None], outgoing, 0)
    arrived = lax.all_to_all(outgoing, "expert", split_axis=1, concat_axis=1, tiled=True)
    lengths = jnp.take(prompt_pages, own_picks)
    new_keys = arrived[:, :, 0].reshape(MAXP, devices * PAGE_TOKENS, key_value_width)
    new_values = arrived[:, :, 1].reshape(MAXP, devices * PAGE_TOKENS, key_value_width)
    new_allowed = (jnp.arange(devices * PAGE_TOKENS, dtype=jnp.int32) // PAGE_TOKENS)[
        None, :
    ] < lengths[:, None]
    fresh_rows = attend(
        queries[:MAXP],
        new_keys,
        new_values,
        new_allowed,
        decode_key_value[:MAXP, 0],
        decode_key_value[:MAXP, 1],
    )
    fetched = local_kv[page_table]
    old_keys = fetched[:, :, 0].reshape(seq_dev, MAXB * PAGE_TOKENS, key_value_width)
    old_values = fetched[:, :, 1].reshape(seq_dev, MAXB * PAGE_TOKENS, key_value_width)
    old_allowed = (jnp.arange(MAXB * PAGE_TOKENS, dtype=jnp.int32) // PAGE_TOKENS)[
        None, :
    ] < seq_blocks[:, None]
    old_out = attend(
        queries, old_keys, old_values, old_allowed, decode_key_value[:, 0], decode_key_value[:, 1]
    )
    new_count = jnp.sum(own_occupied.astype(jnp.int32))
    is_new = jnp.arange(MAXP, dtype=jnp.int32) < new_count
    attention = jnp.concatenate(
        [jnp.where(is_new[:, None], fresh_rows, old_out[:MAXP]), old_out[MAXP:]], 0
    )
    residual = (hidden_in.astype(jnp.float32) + attention.astype(jnp.float32)).astype(jnp.bfloat16)
    resid_wide = residual.astype(jnp.float32)
    normed = (
        resid_wide
        * lax.rsqrt(jnp.mean(resid_wide * resid_wide, -1, keepdims=True) + norm_eps)
        * norm_gain
    ).astype(jnp.bfloat16)
    logits = jnp.dot(normed, router, preferred_element_type=jnp.float32)
    expert_onehot = route_ids[:, :, None] == jnp.arange(experts, dtype=jnp.int32)[None, None, :]
    selected = jnp.sum(jnp.where(expert_onehot, logits[:, None, :], 0.0), -1)
    gate_weights = jax.nn.softmax(selected, -1)
    if capacity >= seq_dev and devices & (devices - 1) == 0:
        spread = jnp.sum(jnp.where(expert_onehot, gate_weights[:, :, None], 0.0), 1)
        return all_tokens(resid_wide, normed, spread, w_gate[0], w_up[0], w_down[0])
    assigned = seq_dev * TOPK
    expert_ids = route_ids.reshape(assigned)
    chosen = (expert_ids[:, None] == jnp.arange(experts, dtype=jnp.int32)[None, :]).astype(
        jnp.int32
    )
    before = jnp.cumsum(chosen, 0) - chosen
    slot_rank = jnp.sum(before * chosen, 1)
    slot_index = expert_ids * capacity + slot_rank
    placing = slot_index[None, :] == jnp.arange(experts * capacity, dtype=jnp.int32)[:, None]
    selector = jnp.any(placing.reshape(experts * capacity, seq_dev, TOPK), -1).astype(jnp.bfloat16)
    gathered_rows = jnp.dot(selector, normed, preferred_element_type=jnp.float32).astype(
        jnp.bfloat16
    )
    outgoing_half = gathered_rows.reshape(devices, half_cap, D)
    own_half = lax.all_to_all(outgoing_half, "expert", split_axis=0, concat_axis=0, tiled=True)
    partner_half = partner(own_half, "expert", 0)
    received = jnp.where(
        even_core,
        jnp.concatenate([own_half, partner_half], 1),
        jnp.concatenate([partner_half, own_half], 1),
    )
    flattened = received.reshape(devices * capacity, D)
    gate_proj = jnp.dot(flattened, w_gate[0], preferred_element_type=jnp.float32)
    up_proj = jnp.dot(flattened, w_up[0], preferred_element_type=jnp.float32)
    activated = (jax.nn.silu(gate_proj) * up_proj).astype(jnp.bfloat16)
    partial_value = jnp.dot(activated, w_down[0], preferred_element_type=jnp.float32).reshape(
        devices, capacity, D
    )
    kept = jnp.where(even_core, partial_value[:, :half_cap], partial_value[:, half_cap:])
    handed = jnp.where(even_core, partial_value[:, half_cap:], partial_value[:, :half_cap])
    partner_part = partner(handed, "expert", 0)
    finished = (kept + partner_part).astype(jnp.bfloat16)
    returned = lax.all_to_all(finished, "expert", split_axis=0, concat_axis=0, tiled=True)
    expert_sum = returned.reshape(experts * capacity, D)
    picked = jnp.take(expert_sum, slot_index, axis=0).astype(jnp.float32).reshape(seq_dev, TOPK, D)
    expert_mix = jnp.sum(picked * gate_weights[:, :, None], 1)
    return (resid_wide + expert_mix).astype(jnp.bfloat16)


def solution(mesh):
    return jax.shard_map(
        local,
        mesh=mesh,
        in_specs=(
            P(("groups", "expert"), None),
            P(("groups", "expert"), None),
            P(("groups", "expert"), None, None),
            P(("groups", "expert"), None, None, None),
            P(("groups", "expert"), None),
            P(("groups", "expert")),
            P(("groups", "expert"), None, None, None, None),
            P("groups"),
            P("groups"),
            P(),
            P(),
            P("expert", None, None),
            P("expert", None, None),
            P("expert", None, None),
            P(("groups", "expert"), None),
        ),
        out_specs=P(("groups", "expert"), None),
        check_vma=False,
    )
```

```python
import functools
import math

import jax
import jax.numpy as jnp
from jax import lax
from jax.experimental import pallas as pl
from jax.experimental.pallas import tpu as pltpu
from jax.sharding import PartitionSpec as P

D = 4096
QUERY_HEADS = 32
KEY_VALUE_HEADS = 2
HEAD_SIZE = 128
PAGE_TOKENS = 16
TOPK = 8
MAXB = 16
MAXP = 2


norm_eps = 1e-06
masked_score = -1e30


def partner(x, axis, apart):
    return lax.ppermute(x, axis, [(i, i ^ 1 << apart) for i in range(lax.axis_size(axis))])


def swap(x, axis, offset):
    return lax.ppermute(x, axis, [(i, i ^ offset) for i in range(lax.axis_size(axis))])


def whole(space):
    return pl.BlockSpec(memory_space=space)


VM, SM = whole(pltpu.VMEM), whole(pltpu.SMEM)
MIB = 1 << 20


def pack_kernel(owner, pages, out, source, count):
    def clear(i, _):
        source[i] = 0
        return 0

    def clear_count(i, _):
        count[i] = 0
        return 0

    def place(p, _):
        o = owner[p]
        r = count[o]
        source[o * MAXP + r] = p
        count[o] = r + 1
        return 0

    def move(i, _):
        out[i] = pages[source[i]]
        return 0

    lax.fori_loop(0, source.shape[0], clear, 0, unroll=8)
    lax.fori_loop(0, count.shape[0], clear_count, 0, unroll=8)
    lax.fori_loop(0, owner.shape[0], place, 0, unroll=8)
    lax.fori_loop(0, out.shape[0], move, 0, unroll=8)


def pack(prompt_owner, pages, devices):
    return pl.pallas_call(
        pack_kernel,
        out_shape=jax.ShapeDtypeStruct((devices * MAXP,) + pages.shape[1:], pages.dtype),
        in_specs=[SM, VM],
        out_specs=VM,
        scratch_shapes=[pltpu.SMEM((devices * MAXP,), jnp.int32), pltpu.SMEM((devices,), jnp.int32)],
        compiler_params=pltpu.CompilerParams(vmem_limit_bytes=16 * MIB),
        name="pack_pages",
    )(prompt_owner, pages)


def pool_attention(wide, keys, values, counts, own_key, own_value):
    group, seqs, size = wide.shape
    scale = 1.0 / math.sqrt(HEAD_SIZE)
    flat = wide.reshape(group * seqs, size).astype(jnp.bfloat16)
    scores = (
        lax.dot_general(flat, keys, (((1,), (1,)), ((), ())), preferred_element_type=jnp.float32)
        * scale
    ).reshape(group, seqs, keys.shape[0])
    allowed = (counts > 0.0)[None]
    scores = jnp.where(allowed, scores, masked_score)
    own_score = jnp.sum(wide * own_key[None], -1, keepdims=True) * scale
    peak = jnp.maximum(jnp.max(scores, -1, keepdims=True), own_score)
    weights = jnp.where(allowed, jnp.exp(scores - peak), 0.0) * counts[None]
    own_weight = jnp.exp(own_score - peak)
    inverse = 1.0 / (jnp.sum(weights, -1, keepdims=True) + own_weight)
    probs = (weights * inverse).astype(jnp.bfloat16).reshape(group * seqs, keys.shape[0])
    own_prob = (own_weight * inverse).astype(jnp.bfloat16).astype(jnp.float32)
    out = jnp.dot(probs, values, preferred_element_type=jnp.float32).reshape(group, seqs, size)
    return out + own_prob * own_value[None]


def head_slabs(queries, g):
    group = QUERY_HEADS // KEY_VALUE_HEADS
    return jnp.concatenate(
        [
            queries[:, (g * group + j) * HEAD_SIZE : (g * group + j + 1) * HEAD_SIZE].astype(
                jnp.float32
            )[None]
            for j in range(group)
        ],
        0,
    )


def local_kernel(blocks, queries, own_kv, pool, table, out):
    seqs = queries.shape[0]
    tokens = pool.shape[0] * PAGE_TOKENS
    page = lax.broadcasted_iota(jnp.int32, (seqs, tokens), 1) // PAGE_TOKENS
    row = lax.broadcasted_iota(jnp.int32, (seqs, 1), 0)
    limit = jnp.zeros((seqs, 1), jnp.int32)
    for s in range(seqs):
        limit = jnp.where(row == s, blocks[s], limit)
    counts = jnp.zeros((seqs, tokens), jnp.float32)
    for b in range(table.shape[1]):
        entry = jnp.where(limit > b, table[:, b : b + 1], -1)
        counts = counts + jnp.where(page == entry, 1.0, 0.0)
    group = QUERY_HEADS // KEY_VALUE_HEADS
    for g in range(KEY_VALUE_HEADS):
        cols = slice(g * HEAD_SIZE, (g + 1) * HEAD_SIZE)
        result = pool_attention(
            head_slabs(queries, g),
            pool[:, 0, :, cols].reshape(tokens, HEAD_SIZE),
            pool[:, 1, :, cols].reshape(tokens, HEAD_SIZE),
            counts,
            own_kv[:, 0, cols].astype(jnp.float32),
            own_kv[:, 1, cols].astype(jnp.float32),
        )
        for j in range(group):
            at = (g * group + j) * HEAD_SIZE
            out[:, at : at + HEAD_SIZE] = result[j].astype(jnp.bfloat16)


def local_attention(seq_blocks, queries, own_kv, pool, page_table):
    return pl.pallas_call(
        local_kernel,
        out_shape=jax.ShapeDtypeStruct(queries.shape, jnp.bfloat16),
        in_specs=[SM, VM, VM, VM, VM],
        out_specs=VM,
        compiler_params=pltpu.CompilerParams(vmem_limit_bytes=16 * MIB),
        name="local_attention",
    )(seq_blocks, queries, own_kv, pool, page_table)


def head_kernel(
    tail, position, owner, lengths, queries, own_kv, arrived, old, hidden, gain, router, routes,
    residual, payload, spread, mixed,
):
    seqs = queries.shape[0]
    width = queries.shape[1]
    experts = router.shape[1]
    tokens = arrived.shape[0] * PAGE_TOKENS
    here = position[0]

    def find(p, carry):
        found = carry[0]
        mine = owner[p] == here
        picked = [
            jnp.where(mine & (found == r), lengths[p], carry[1 + r]) for r in range(MAXP)
        ]
        return (jnp.where(mine, found + 1, found), *picked)

    state = lax.fori_loop(
        0, owner.shape[0], find, (jnp.int32(0),) * (1 + MAXP), unroll=8
    )
    new_count = state[0]
    row = lax.broadcasted_iota(jnp.int32, (seqs, 1), 0)
    page = lax.broadcasted_iota(jnp.int32, (seqs, tokens), 1) // PAGE_TOKENS
    counts = jnp.concatenate(
        [
            jnp.where((page < state[1 + r]) & (row == r), 1.0, 0.0)
            for r in range(MAXP)
        ],
        1,
    )
    is_new = row < new_count
    group = QUERY_HEADS // KEY_VALUE_HEADS
    for g in range(KEY_VALUE_HEADS):
        cols = slice(g * HEAD_SIZE, (g + 1) * HEAD_SIZE)

        def side(kv):
            return jnp.concatenate(
                [arrived[:, r, kv, :, cols].reshape(tokens, HEAD_SIZE) for r in range(MAXP)], 0
            )

        result = pool_attention(
            head_slabs(queries, g),
            side(0),
            side(1),
            counts,
            own_kv[:, 0, cols].astype(jnp.float32),
            own_kv[:, 1, cols].astype(jnp.float32),
        )
        for j in range(group):
            at = slice((g * group + j) * HEAD_SIZE, (g * group + j + 1) * HEAD_SIZE)
            fresh = result[j].astype(jnp.bfloat16).astype(jnp.float32)
            chosen = jnp.where(is_new, fresh, old[:, at].astype(jnp.float32))
            mixed[:, at] = hidden[:, at].astype(jnp.float32) + chosen
    summed = mixed[...].astype(jnp.bfloat16)
    residual[...] = summed
    wide = summed.astype(jnp.float32)
    level = lax.rsqrt(jnp.mean(wide * wide, -1, keepdims=True) + norm_eps)
    normed = (wide * level * gain[...]).astype(jnp.bfloat16)
    payload[:, :width] = normed
    logits = jnp.dot(normed, router[...], preferred_element_type=jnp.float32)
    lane = lax.broadcasted_iota(jnp.int32, (seqs, experts), 1)
    chosen = jnp.zeros((seqs, experts), jnp.float32)
    for k in range(routes.shape[1]):
        chosen = chosen + jnp.where(routes[:, k : k + 1] == lane, 1.0, 0.0)
    top = jnp.max(jnp.where(chosen > 0.0, logits, masked_score), -1, keepdims=True)
    powers = jnp.where(chosen > 0.0, jnp.exp(logits - top), 0.0) * chosen
    gates = powers / jnp.sum(powers, -1, keepdims=True)
    spread[...] = gates
    if tail:
        payload[:, width:] = jnp.zeros((seqs, tail), jnp.bfloat16)
        coarse = gates.astype(jnp.bfloat16)
        payload[:, width : width + experts] = coarse
        fine = (gates - coarse.astype(jnp.float32)).astype(jnp.bfloat16)
        payload[:, width + tail // 2 : width + tail // 2 + experts] = fine


def finish_heads(
    tail, position, prompt_owner, prompt_pages, queries, own_kv, arrived, old, hidden, gain, router, routes
):
    seqs, width = queries.shape
    return pl.pallas_call(
        functools.partial(head_kernel, tail),
        out_shape=(
            jax.ShapeDtypeStruct((seqs, width), jnp.bfloat16),
            jax.ShapeDtypeStruct((seqs, width + tail), jnp.bfloat16),
            jax.ShapeDtypeStruct((seqs, router.shape[1]), jnp.float32),
        ),
        in_specs=[SM, SM, SM] + [VM] * 8,
        out_specs=(VM, VM, VM),
        scratch_shapes=[pltpu.VMEM((seqs, width), jnp.float32)],
        compiler_params=pltpu.CompilerParams(vmem_limit_bytes=32 * MIB),
        name="finish_heads",
    )(
        position, prompt_owner, prompt_pages, queries, own_kv, arrived, old, hidden, gain, router, routes
    )


def expert_kernel(
    tail, expert, near, across, core_near, core_across, w_gate, w_up, w_down,
    near_out, across_out, core_near_out, core_across_out,
):
    width = w_gate.shape[0]
    share = near.shape[0]
    blocks = (near, across, core_near, core_across)
    tokens = jnp.concatenate([block[:, :width] for block in blocks], 0)
    ends = jnp.concatenate([block[:, width:].astype(jnp.float32) for block in blocks], 0)
    lane = lax.broadcasted_iota(jnp.int32, ends.shape, 1)
    wanted = (lane == expert[0]) | (lane == expert[0] + tail // 2)
    gate = jnp.sum(jnp.where(wanted, ends, 0.0), -1, keepdims=True)
    gate_proj = jnp.dot(tokens, w_gate[...], preferred_element_type=jnp.float32)
    up_proj = jnp.dot(tokens, w_up[...], preferred_element_type=jnp.float32)
    activated = (gate_proj / (1.0 + jnp.exp(-gate_proj)) * up_proj).astype(jnp.bfloat16)
    step = min(width, 1024)
    for at in range(0, width, step):
        cols = slice(at, at + step)
        part = jnp.dot(activated, w_down[:, cols], preferred_element_type=jnp.float32) * gate
        core_across_out[:, cols] = part[3 * share :].astype(jnp.bfloat16)
        core_near_out[:, cols] = part[2 * share : 3 * share].astype(jnp.bfloat16)
        across_out[:, cols] = part[share : 2 * share]
        near_out[:, cols] = part[:share]


def expert_half(tail, expert, blocks, w_gate, w_up, w_down):
    share, width = blocks[0].shape[0], w_gate.shape[0]
    wide = jax.ShapeDtypeStruct((share, width), jnp.float32)
    sent = jax.ShapeDtypeStruct((share, width), jnp.bfloat16)
    return pl.pallas_call(
        functools.partial(expert_kernel, tail),
        out_shape=(wide, wide, sent, sent),
        in_specs=[SM] + [VM] * 7,
        out_specs=(VM,) * 4,
        compiler_params=pltpu.CompilerParams(vmem_limit_bytes=40 * MIB),
        name="expert_half",
    )(expert, *blocks, w_gate, w_up, w_down)


def all_tokens(tail, residual, payload, position, w_gate, w_up, w_down):
    seqs = payload.shape[0]
    devices = lax.axis_size("expert")
    far = range(4, devices, 4)
    near = jnp.concatenate([payload] + [swap(payload, "expert", f) for f in far], 0)
    across = swap(near, "expert", 2)
    core_near = swap(near, "expert", 1)
    core_across = swap(across, "expert", 1)
    expert = position // 2
    near_sum, across_sum, core_near_part, core_across_part = expert_half(
        tail, expert, (near, across, core_near, core_across), w_gate, w_up, w_down
    )
    across_sum = across_sum + swap(core_across_part, "expert", 1).astype(jnp.float32)
    near_sum = near_sum + swap(core_near_part, "expert", 1).astype(jnp.float32)
    near_sum = near_sum + swap(across_sum.astype(jnp.bfloat16), "expert", 2).astype(jnp.float32)
    total = residual.astype(jnp.float32) + near_sum[:seqs]
    for at, f in enumerate(far):
        piece = near_sum[(at + 1) * seqs : (at + 2) * seqs].astype(jnp.bfloat16)
        total = total + swap(piece, "expert", f).astype(jnp.float32)
    return total.astype(jnp.bfloat16)


def local(
    hidden_in,
    queries,
    decode_key_value,
    local_kv,
    page_table,
    seq_blocks,
    prompt_kv,
    prompt_owner,
    prompt_pages,
    norm_gain,
    router,
    w_gate,
    w_up,
    w_down,
    route_ids,
):
    devices = lax.axis_size("expert")
    position = lax.axis_index("expert")
    experts = devices // 2
    seq_dev = hidden_in.shape[0]
    key_value_width = KEY_VALUE_HEADS * HEAD_SIZE
    capacity = min(seq_dev, max(2, 2 * ((3 * seq_dev * TOPK + 2 * devices - 1) // (2 * devices))))
    half_cap = capacity // 2
    even_core = position % 2 == 0
    dense = capacity >= seq_dev and devices >= 4 and devices & (devices - 1) == 0
    tail = 2 * (-(-experts // 64) * 64) if dense else 0
    here = position.astype(jnp.int32).reshape(1)
    outgoing = pack(prompt_owner, prompt_kv[0], devices)
    arrived = lax.all_to_all(
        outgoing.reshape(devices, MAXP, 2, PAGE_TOKENS, key_value_width),
        "expert",
        split_axis=0,
        concat_axis=0,
        tiled=True,
    )
    old = local_attention(seq_blocks, queries, decode_key_value, local_kv, page_table)
    residual, normed, spread = finish_heads(
        tail,
        here,
        prompt_owner,
        prompt_pages,
        queries,
        decode_key_value,
        arrived,
        old,
        hidden_in,
        norm_gain.reshape(1, D),
        router,
        route_ids,
    )
    if dense:
        return all_tokens(tail, residual, normed, here, w_gate[0], w_up[0], w_down[0])
    resid_wide = residual.astype(jnp.float32)
    expert_onehot = route_ids[:, :, None] == jnp.arange(experts, dtype=jnp.int32)[None, None, :]
    gate_weights = jnp.sum(jnp.where(expert_onehot, spread[:, None, :], 0.0), -1)
    assigned = seq_dev * TOPK
    expert_ids = route_ids.reshape(assigned)
    chosen = (expert_ids[:, None] == jnp.arange(experts, dtype=jnp.int32)[None, :]).astype(
        jnp.int32
    )
    before = jnp.cumsum(chosen, 0) - chosen
    slot_rank = jnp.sum(before * chosen, 1)
    slot_index = expert_ids * capacity + slot_rank
    placing = slot_index[None, :] == jnp.arange(experts * capacity, dtype=jnp.int32)[:, None]
    selector = jnp.any(placing.reshape(experts * capacity, seq_dev, TOPK), -1).astype(jnp.bfloat16)
    gathered_rows = jnp.dot(selector, normed, preferred_element_type=jnp.float32).astype(
        jnp.bfloat16
    )
    outgoing_half = gathered_rows.reshape(devices, half_cap, D)
    own_half = lax.all_to_all(outgoing_half, "expert", split_axis=0, concat_axis=0, tiled=True)
    partner_half = partner(own_half, "expert", 0)
    received = jnp.where(
        even_core,
        jnp.concatenate([own_half, partner_half], 1),
        jnp.concatenate([partner_half, own_half], 1),
    )
    flattened = received.reshape(devices * capacity, D)
    gate_proj = jnp.dot(flattened, w_gate[0], preferred_element_type=jnp.float32)
    up_proj = jnp.dot(flattened, w_up[0], preferred_element_type=jnp.float32)
    activated = (jax.nn.silu(gate_proj) * up_proj).astype(jnp.bfloat16)
    partial_value = jnp.dot(activated, w_down[0], preferred_element_type=jnp.float32).reshape(
        devices, capacity, D
    )
    kept = jnp.where(even_core, partial_value[:, :half_cap], partial_value[:, half_cap:])
    handed = jnp.where(even_core, partial_value[:, half_cap:], partial_value[:, :half_cap])
    partner_part = partner(handed, "expert", 0)
    finished = (kept + partner_part).astype(jnp.bfloat16)
    returned = lax.all_to_all(finished, "expert", split_axis=0, concat_axis=0, tiled=True)
    expert_sum = returned.reshape(experts * capacity, D)
    picked = jnp.take(expert_sum, slot_index, axis=0).astype(jnp.float32).reshape(seq_dev, TOPK, D)
    expert_mix = jnp.sum(picked * gate_weights[:, :, None], 1)
    return (resid_wide + expert_mix).astype(jnp.bfloat16)


def solution(mesh):
    return jax.shard_map(
        local,
        mesh=mesh,
        in_specs=(
            P(("groups", "expert"), None),
            P(("groups", "expert"), None),
            P(("groups", "expert"), None, None),
            P(("groups", "expert"), None, None, None),
            P(("groups", "expert"), None),
            P(("groups", "expert")),
            P(("groups", "expert"), None, None, None, None),
            P("groups"),
            P("groups"),
            P(),
            P(),
            P("expert", None, None),
            P("expert", None, None),
            P("expert", None, None),
            P(("groups", "expert"), None),
        ),
        out_specs=P(("groups", "expert"), None),
        check_vma=False,
    )
```

```python
import functools
import math

import jax
import jax.numpy as jnp
from jax import lax
from jax.experimental import pallas as pl
from jax.experimental.pallas import tpu as pltpu
from jax.sharding import PartitionSpec as P

D = 4096
QUERY_HEADS = 32
KEY_VALUE_HEADS = 2
HEAD_SIZE = 128
PAGE_TOKENS = 16
TOPK = 8
MAXB = 16
MAXP = 2


norm_eps = 1e-06
masked_score = -1e30


def partner(x, axis, apart):
    return lax.ppermute(x, axis, [(i, i ^ 1 << apart) for i in range(lax.axis_size(axis))])


def swap(x, axis, offset):
    return lax.ppermute(x, axis, [(i, i ^ offset) for i in range(lax.axis_size(axis))])


def whole(space):
    return pl.BlockSpec(memory_space=space)


VM, SM, ANY = whole(pltpu.VMEM), whole(pltpu.SMEM), whole(pl.ANY)
MIB = 1 << 20


def pack_kernel(owner_in, pages_in, out, owner, pages, source, count, sems):
    fetch_owner = pltpu.make_async_copy(owner_in, owner, sems.at[0])
    fetch_pages = pltpu.make_async_copy(pages_in, pages, sems.at[1])
    fetch_owner.start()
    fetch_pages.start()

    def clear(i, _):
        source[i] = 0
        return 0

    def clear_count(i, _):
        count[i] = 0
        return 0

    def place(p, _):
        o = owner[p]
        r = count[o]
        source[o * MAXP + r] = p
        count[o] = r + 1
        return 0

    def move(i, _):
        out[i] = pages[source[i]]
        return 0

    lax.fori_loop(0, source.shape[0], clear, 0, unroll=8)
    lax.fori_loop(0, count.shape[0], clear_count, 0, unroll=8)
    fetch_owner.wait()
    lax.fori_loop(0, owner.shape[0], place, 0, unroll=8)
    fetch_pages.wait()
    lax.fori_loop(0, out.shape[0], move, 0, unroll=8)


def pack(prompt_owner, pages, devices):
    return pl.pallas_call(
        pack_kernel,
        out_shape=jax.ShapeDtypeStruct((devices * MAXP,) + pages.shape[1:], pages.dtype),
        in_specs=[ANY, ANY],
        out_specs=VM,
        scratch_shapes=[
            pltpu.SMEM(prompt_owner.shape, jnp.int32),
            pltpu.VMEM(pages.shape, pages.dtype),
            pltpu.SMEM((devices * MAXP,), jnp.int32),
            pltpu.SMEM((devices,), jnp.int32),
            pltpu.SemaphoreType.DMA((2,)),
        ],
        compiler_params=pltpu.CompilerParams(vmem_limit_bytes=16 * MIB),
        name="pack_pages",
    )(prompt_owner, pages)


def pool_attention(wide, keys, values, counts, own_key, own_value):
    group, seqs, size = wide.shape
    scale = 1.0 / math.sqrt(HEAD_SIZE)
    flat = wide.reshape(group * seqs, size).astype(jnp.bfloat16)
    scores = (
        lax.dot_general(flat, keys, (((1,), (1,)), ((), ())), preferred_element_type=jnp.float32)
        * scale
    ).reshape(group, seqs, keys.shape[0])
    allowed = (counts > 0.0)[None]
    scores = jnp.where(allowed, scores, masked_score)
    own_score = jnp.sum(wide * own_key[None], -1, keepdims=True) * scale
    peak = jnp.maximum(jnp.max(scores, -1, keepdims=True), own_score)
    weights = jnp.where(allowed, jnp.exp(scores - peak), 0.0) * counts[None]
    own_weight = jnp.exp(own_score - peak)
    inverse = 1.0 / (jnp.sum(weights, -1, keepdims=True) + own_weight)
    probs = (weights * inverse).astype(jnp.bfloat16).reshape(group * seqs, keys.shape[0])
    own_prob = (own_weight * inverse).astype(jnp.bfloat16).astype(jnp.float32)
    out = jnp.dot(probs, values, preferred_element_type=jnp.float32).reshape(group, seqs, size)
    return out + own_prob * own_value[None]


def head_slabs(queries, g):
    group = QUERY_HEADS // KEY_VALUE_HEADS
    return jnp.concatenate(
        [
            queries[:, (g * group + j) * HEAD_SIZE : (g * group + j + 1) * HEAD_SIZE].astype(
                jnp.float32
            )[None]
            for j in range(group)
        ],
        0,
    )


def own_prompts(position, owner, lengths):
    here = position[0]

    def find(p, carry):
        found = carry[0]
        mine = owner[p] == here
        picked = [jnp.where(mine & (found == r), lengths[p], carry[1 + r]) for r in range(MAXP)]
        return (jnp.where(mine, found + 1, found), *picked)

    state = lax.fori_loop(0, owner.shape[0], find, (jnp.int32(0),) * (1 + MAXP), unroll=8)
    return state[0], state[1:]


def normalize(tail, mixed, keep, gain, router, routes, residual, payload, spread):
    seqs, width = mixed.shape
    rows = residual.shape[0]
    experts = router.shape[1]
    summed = mixed[...].astype(jnp.bfloat16)
    wide = summed.astype(jnp.float32)
    residual[...] = jnp.where(keep, wide, 0.0).astype(jnp.bfloat16)[:rows]
    level = lax.rsqrt(jnp.mean(wide * wide, -1, keepdims=True) + norm_eps)
    normed = (wide * level * gain[...]).astype(jnp.bfloat16)
    payload[:, :width] = normed[:rows]
    logits = jnp.dot(normed, router[...], preferred_element_type=jnp.float32)
    lane = lax.broadcasted_iota(jnp.int32, (seqs, experts), 1)
    chosen = jnp.zeros((seqs, experts), jnp.float32)
    for k in range(routes.shape[1]):
        chosen = chosen + jnp.where(routes[:, k : k + 1] == lane, 1.0, 0.0)
    top = jnp.max(jnp.where(chosen > 0.0, logits, masked_score), -1, keepdims=True)
    powers = jnp.where(chosen > 0.0, jnp.exp(logits - top), 0.0) * chosen
    gates = jnp.where(keep, powers / jnp.sum(powers, -1, keepdims=True), 0.0)
    spread[...] = gates[:rows]
    if tail:
        payload[:, width:] = jnp.zeros((rows, tail), jnp.bfloat16)
        coarse = gates.astype(jnp.bfloat16)
        fine = (gates - coarse.astype(jnp.float32)).astype(jnp.bfloat16)
        payload[:, width : width + experts] = coarse[:rows]
        payload[:, width + tail // 2 : width + tail // 2 + experts] = fine[:rows]


def old_kernel(
    tail, position, owner, lengths, blocks, queries, own_kv, pool, table, hidden, gain, router, routes,
    residual, payload, spread, mixed,
):
    seqs = queries.shape[0]
    tokens = pool.shape[0] * PAGE_TOKENS
    new_count, _ = own_prompts(position, owner, lengths)
    page = lax.broadcasted_iota(jnp.int32, (seqs, tokens), 1) // PAGE_TOKENS
    row = lax.broadcasted_iota(jnp.int32, (seqs, 1), 0)
    limit = jnp.zeros((seqs, 1), jnp.int32)
    for s in range(seqs):
        limit = jnp.where(row == s, blocks[s], limit)
    counts = jnp.zeros((seqs, tokens), jnp.float32)
    for b in range(table.shape[1]):
        entry = jnp.where(limit > b, table[:, b : b + 1], -1)
        counts = counts + jnp.where(page == entry, 1.0, 0.0)
    group = QUERY_HEADS // KEY_VALUE_HEADS
    for g in range(KEY_VALUE_HEADS):
        cols = slice(g * HEAD_SIZE, (g + 1) * HEAD_SIZE)
        result = pool_attention(
            head_slabs(queries, g),
            pool[:, 0, :, cols].reshape(tokens, HEAD_SIZE),
            pool[:, 1, :, cols].reshape(tokens, HEAD_SIZE),
            counts,
            own_kv[:, 0, cols].astype(jnp.float32),
            own_kv[:, 1, cols].astype(jnp.float32),
        )
        for j in range(group):
            at = slice((g * group + j) * HEAD_SIZE, (g * group + j + 1) * HEAD_SIZE)
            rounded = result[j].astype(jnp.bfloat16).astype(jnp.float32)
            mixed[:, at] = hidden[:, at].astype(jnp.float32) + rounded
    normalize(tail, mixed, row >= new_count, gain, router, routes, residual, payload, spread)


def fresh_kernel(
    tail, position, owner, lengths, queries, own_kv, arrived, hidden, gain, router, routes,
    residual, payload, spread, mixed,
):
    seqs = queries.shape[0]
    tokens = arrived.shape[0] * PAGE_TOKENS
    new_count, pages = own_prompts(position, owner, lengths)
    row = lax.broadcasted_iota(jnp.int32, (seqs, 1), 0)
    page = lax.broadcasted_iota(jnp.int32, (seqs, tokens), 1) // PAGE_TOKENS
    counts = jnp.concatenate(
        [jnp.where((page < pages[r]) & (row == r), 1.0, 0.0) for r in range(MAXP)], 1
    )
    group = QUERY_HEADS // KEY_VALUE_HEADS
    for g in range(KEY_VALUE_HEADS):
        cols = slice(g * HEAD_SIZE, (g + 1) * HEAD_SIZE)

        def side(kv):
            return jnp.concatenate(
                [arrived[:, r, kv, :, cols].reshape(tokens, HEAD_SIZE) for r in range(MAXP)], 0
            )

        result = pool_attention(
            head_slabs(queries, g),
            side(0),
            side(1),
            counts,
            own_kv[:, 0, cols].astype(jnp.float32),
            own_kv[:, 1, cols].astype(jnp.float32),
        )
        for j in range(group):
            at = slice((g * group + j) * HEAD_SIZE, (g * group + j + 1) * HEAD_SIZE)
            rounded = result[j].astype(jnp.bfloat16).astype(jnp.float32)
            mixed[:, at] = hidden[:, at].astype(jnp.float32) + rounded
    normalize(tail, mixed, row < new_count, gain, router, routes, residual, payload, spread)


def heads(kernel, name, tail, rows, experts, scalars, arrays):
    seqs, width = arrays[0].shape
    return pl.pallas_call(
        functools.partial(kernel, tail),
        out_shape=(
            jax.ShapeDtypeStruct((rows, width), jnp.bfloat16),
            jax.ShapeDtypeStruct((rows, width + tail), jnp.bfloat16),
            jax.ShapeDtypeStruct((rows, experts), jnp.float32),
        ),
        in_specs=[SM] * len(scalars) + [VM] * len(arrays),
        out_specs=(VM, VM, VM),
        scratch_shapes=[pltpu.VMEM((seqs, width), jnp.float32)],
        compiler_params=pltpu.CompilerParams(vmem_limit_bytes=32 * MIB),
        name=name,
    )(*scalars, *arrays)


def expert_rows(tail, expert, blocks, gate_up, down, outs):
    near_out, across_out, core_near_out, core_across_out = outs
    share, width = near_out.shape
    ends = jnp.concatenate([block[:, width:].astype(jnp.float32) for block in blocks], 0)
    lane = lax.broadcasted_iota(jnp.int32, ends.shape, 1)
    wanted = (lane == expert[0]) | (lane == expert[0] + tail // 2)
    gate = jnp.sum(jnp.where(wanted, ends, 0.0), -1, keepdims=True)
    gate_proj, up_proj = gate_up(
        lambda cols: jnp.concatenate([block[:, cols] for block in blocks], 0)
    )
    activated = (gate_proj / (1.0 + jnp.exp(-gate_proj)) * up_proj).astype(jnp.bfloat16)
    step = min(width, 1024)
    for at in range(0, width, step):
        cols = slice(at, at + step)
        part = jnp.dot(activated, down(cols), preferred_element_type=jnp.float32) * gate
        core_across_out[:, cols] = part[3 * share :].astype(jnp.bfloat16)
        core_near_out[:, cols] = part[2 * share : 3 * share].astype(jnp.bfloat16)
        across_out[:, cols] = part[share : 2 * share]
        near_out[:, cols] = part[:share]


PIECES = 4


def first_expert_kernel(
    tail, expert, near, across, core_near, core_across, gate_in, up_in, down_in,
    near_out, across_out, core_near_out, core_across_out, w_gate, w_up, w_down, sems,
):
    width, hidden = w_gate.shape
    part = width // PIECES
    copies = {}
    for at in range(PIECES):
        rows = pl.ds(at * part, part)
        for i, (src, dst) in enumerate(((gate_in, w_gate), (up_in, w_up))):
            copies[i, at] = pltpu.make_async_copy(src.at[rows], dst.at[rows], sems.at[i, at])
    for at in range(PIECES):
        rows = pl.ds(at * (hidden // PIECES), hidden // PIECES)
        copies[2, at] = pltpu.make_async_copy(down_in.at[rows], w_down.at[rows], sems.at[2, at])
    for copy in copies.values():
        copy.start()

    def gate_up(tokens):
        gate_proj = up_proj = 0.0
        for at in range(PIECES):
            cols = slice(at * part, (at + 1) * part)
            x = tokens(cols)
            copies[0, at].wait()
            gate_proj = gate_proj + jnp.dot(x, w_gate[cols], preferred_element_type=jnp.float32)
            copies[1, at].wait()
            up_proj = up_proj + jnp.dot(x, w_up[cols], preferred_element_type=jnp.float32)
        for at in range(PIECES):
            copies[2, at].wait()
        return gate_proj, up_proj

    expert_rows(
        tail, expert, (near, across, core_near, core_across), gate_up,
        lambda cols: w_down[:, cols],
        (near_out, across_out, core_near_out, core_across_out),
    )


def later_expert_kernel(
    tail, expert, near, across, core_near, core_across, w_gate, w_up, w_down,
    near_out, across_out, core_near_out, core_across_out,
):
    def gate_up(tokens):
        x = tokens(slice(0, w_gate.shape[0]))
        return (
            jnp.dot(x, w_gate[...], preferred_element_type=jnp.float32),
            jnp.dot(x, w_up[...], preferred_element_type=jnp.float32),
        )

    expert_rows(
        tail, expert, (near, across, core_near, core_across), gate_up,
        lambda cols: w_down[:, cols],
        (near_out, across_out, core_near_out, core_across_out),
    )


def expert_half(first, tail, expert, blocks, weights):
    share, width = blocks[0].shape[0], weights[0].shape[0]
    wide = jax.ShapeDtypeStruct((share, width), jnp.float32)
    sent = jax.ShapeDtypeStruct((share, width), jnp.bfloat16)
    kept = tuple(jax.ShapeDtypeStruct(w.shape, w.dtype) for w in weights) if first else ()
    return pl.pallas_call(
        functools.partial(first_expert_kernel if first else later_expert_kernel, tail),
        out_shape=(wide, wide, sent, sent) + kept,
        in_specs=[SM] + [VM] * 4 + [ANY if first else VM] * 3,
        out_specs=(VM,) * (4 + len(kept)),
        scratch_shapes=[pltpu.SemaphoreType.DMA((3, PIECES))] if first else [],
        compiler_params=pltpu.CompilerParams(vmem_limit_bytes=32 * MIB),
        name="first_expert" if first else "later_expert",
    )(expert, *blocks, *weights)


def far_peers():
    return range(4, lax.axis_size("expert"), 4)


def gather_tokens(payload):
    near = jnp.concatenate([payload] + [swap(payload, "expert", f) for f in far_peers()], 0)
    across = swap(near, "expert", 2)
    core_near = swap(near, "expert", 1)
    core_across = swap(across, "expert", 1)
    return near, across, core_near, core_across


def scatter_sums(residual, near_sum, across_sum, core_near_part, core_across_part):
    seqs = residual.shape[0]
    across_sum = across_sum + swap(core_across_part, "expert", 1).astype(jnp.float32)
    near_sum = near_sum + swap(core_near_part, "expert", 1).astype(jnp.float32)
    near_sum = near_sum + swap(across_sum.astype(jnp.bfloat16), "expert", 2).astype(jnp.float32)
    total = residual.astype(jnp.float32) + near_sum[:seqs]
    for at, f in enumerate(far_peers()):
        piece = near_sum[(at + 1) * seqs : (at + 2) * seqs].astype(jnp.bfloat16)
        total = total + swap(piece, "expert", f).astype(jnp.float32)
    return total


def local(
    hidden_in,
    queries,
    decode_key_value,
    local_kv,
    page_table,
    seq_blocks,
    prompt_kv,
    prompt_owner,
    prompt_pages,
    norm_gain,
    router,
    w_gate,
    w_up,
    w_down,
    route_ids,
):
    devices = lax.axis_size("expert")
    position = lax.axis_index("expert")
    experts = devices // 2
    seq_dev = hidden_in.shape[0]
    key_value_width = KEY_VALUE_HEADS * HEAD_SIZE
    capacity = min(seq_dev, max(2, 2 * ((3 * seq_dev * TOPK + 2 * devices - 1) // (2 * devices))))
    half_cap = capacity // 2
    even_core = position % 2 == 0
    dense = capacity >= seq_dev and devices >= 4 and devices & (devices - 1) == 0
    tail = 2 * (-(-experts // 64) * 64) if dense else 0
    here = position.astype(jnp.int32).reshape(1)
    outgoing = pack(prompt_owner, prompt_kv[0], devices)
    arrived = lax.all_to_all(
        outgoing.reshape(devices, MAXP, 2, PAGE_TOKENS, key_value_width),
        "expert",
        split_axis=0,
        concat_axis=0,
        tiled=True,
    )
    scalars = (here, prompt_owner, prompt_pages)
    gain = norm_gain.reshape(1, D)
    old_residual, old_rows, old_spread = heads(
        old_kernel,
        "old_heads",
        tail,
        seq_dev,
        experts,
        scalars + (seq_blocks,),
        (queries, decode_key_value, local_kv, page_table, hidden_in, gain, router, route_ids),
    )
    new_residual, new_rows, new_spread = heads(
        fresh_kernel,
        "new_heads",
        tail,
        MAXP,
        experts,
        scalars,
        (queries, decode_key_value, arrived, hidden_in, gain, router, route_ids),
    )
    if dense:
        expert = here // 2
        old_parts = expert_half(
            True, tail, expert, gather_tokens(old_rows), (w_gate[0], w_up[0], w_down[0])
        )
        new_parts = expert_half(False, tail, expert, gather_tokens(new_rows), old_parts[4:])
        old_total = scatter_sums(old_residual, *old_parts[:4])
        new_total = scatter_sums(new_residual, *new_parts)
        return (old_total + jnp.pad(new_total, ((0, seq_dev - MAXP), (0, 0)))).astype(jnp.bfloat16)
    rest = ((0, seq_dev - MAXP), (0, 0))
    new_count = jnp.sum((prompt_owner == position).astype(jnp.int32))
    is_new = jnp.arange(seq_dev, dtype=jnp.int32)[:, None] < new_count
    residual = old_residual + jnp.pad(new_residual, rest)
    normed = jnp.where(is_new, jnp.pad(new_rows, rest), old_rows)
    spread = old_spread + jnp.pad(new_spread, rest)
    resid_wide = residual.astype(jnp.float32)
    expert_onehot = route_ids[:, :, None] == jnp.arange(experts, dtype=jnp.int32)[None, None, :]
    gate_weights = jnp.sum(jnp.where(expert_onehot, spread[:, None, :], 0.0), -1)
    assigned = seq_dev * TOPK
    expert_ids = route_ids.reshape(assigned)
    chosen = (expert_ids[:, None] == jnp.arange(experts, dtype=jnp.int32)[None, :]).astype(
        jnp.int32
    )
    before = jnp.cumsum(chosen, 0) - chosen
    slot_rank = jnp.sum(before * chosen, 1)
    slot_index = expert_ids * capacity + slot_rank
    placing = slot_index[None, :] == jnp.arange(experts * capacity, dtype=jnp.int32)[:, None]
    selector = jnp.any(placing.reshape(experts * capacity, seq_dev, TOPK), -1).astype(jnp.bfloat16)
    gathered_rows = jnp.dot(selector, normed, preferred_element_type=jnp.float32).astype(
        jnp.bfloat16
    )
    outgoing_half = gathered_rows.reshape(devices, half_cap, D)
    own_half = lax.all_to_all(outgoing_half, "expert", split_axis=0, concat_axis=0, tiled=True)
    partner_half = partner(own_half, "expert", 0)
    received = jnp.where(
        even_core,
        jnp.concatenate([own_half, partner_half], 1),
        jnp.concatenate([partner_half, own_half], 1),
    )
    flattened = received.reshape(devices * capacity, D)
    gate_proj = jnp.dot(flattened, w_gate[0], preferred_element_type=jnp.float32)
    up_proj = jnp.dot(flattened, w_up[0], preferred_element_type=jnp.float32)
    activated = (jax.nn.silu(gate_proj) * up_proj).astype(jnp.bfloat16)
    partial_value = jnp.dot(activated, w_down[0], preferred_element_type=jnp.float32).reshape(
        devices, capacity, D
    )
    kept = jnp.where(even_core, partial_value[:, :half_cap], partial_value[:, half_cap:])
    handed = jnp.where(even_core, partial_value[:, half_cap:], partial_value[:, :half_cap])
    partner_part = partner(handed, "expert", 0)
    finished = (kept + partner_part).astype(jnp.bfloat16)
    returned = lax.all_to_all(finished, "expert", split_axis=0, concat_axis=0, tiled=True)
    expert_sum = returned.reshape(experts * capacity, D)
    picked = jnp.take(expert_sum, slot_index, axis=0).astype(jnp.float32).reshape(seq_dev, TOPK, D)
    expert_mix = jnp.sum(picked * gate_weights[:, :, None], 1)
    return (resid_wide + expert_mix).astype(jnp.bfloat16)


def solution(mesh):
    return jax.shard_map(
        local,
        mesh=mesh,
        in_specs=(
            P(("groups", "expert"), None),
            P(("groups", "expert"), None),
            P(("groups", "expert"), None, None),
            P(("groups", "expert"), None, None, None),
            P(("groups", "expert"), None),
            P(("groups", "expert")),
            P(("groups", "expert"), None, None, None, None),
            P("groups"),
            P("groups"),
            P(),
            P(),
            P("expert", None, None),
            P("expert", None, None),
            P("expert", None, None),
            P(("groups", "expert"), None),
        ),
        out_specs=P(("groups", "expert"), None),
        check_vma=False,
    )
```
